32 devices in a mesh: view: 2 (over x), tile: 16 (over z, y, core).
Axes of the slice: x: 2, y: 2, z: 4, core: 2. Of those that a mesh axis runs over, the one named last changes fastest.
Arguments:
- estimate: float32 [16, 512, 1024], P(None, 'tile', 'view'), may hold values from 0.5 to 2
- measured: bfloat16 [2, 16, 512, 1024], P('view', None, 'tile'), may hold values from 0.05 to 12
- psf_z: float32 [2, 65], P('view'), may hold values from 0.05 to 1
- psf_xy: float32 [2, 2, 9], P('view'), may hold values from 0.1 to 1
- offsets: int32 [2, 2], P('view'), may hold values from -4 to 4, as said below
- coverage: int32 [2, 16], P('view', 'tile'), may hold values from 0 to 1, as said below
Outputs:
- restored: float32 [16, 512, 1024], P(None, 'tile', 'view')
The draws below stay inside these ranges and needn't reach their ends.
Inputs may be any that keep to these rules, and one draw needn't show every extreme that they name: offsets[v, 0] shifts view v along rows and offsets[v, 1] along columns; some view has a row offset of 4 and some view a column offset of -4. coverage[v, t] is 1 where view v images rows t * 32 to (t + 1) * 32 - 1, else 0; every tile is imaged by at least one view.
All inputs are finite; a program needn't handle non-finite values.
Results may differ from the reference program's by a relative error of at most 0.0006.
Values may be sent and summed in bfloat16 or wider, within the bound.
No kernel may reach another device: no remote copies, remote signals or barrier semaphores. Data moves between devices by JAX's collectives and lax.ppermute only.
A program may use at most 64 MiB of HBM per device.

```python
import math
import jax
import jax.numpy as jnp
from jax import lax

NZ = 16
TY = 32
NXT = 1024
RZ = 32
SHIFT = 4
ITERS = 2
VIEWS = 2
TILES = 16
NY = 512
KZ = 65
KXY = 9


def draw_estimate(key, part):
    first_key = jax.random.fold_in(jax.random.fold_in(key, 53), 0)
    values = jnp.exp(jax.random.uniform(first_key, (NZ, NY, NXT), jnp.float32, math.log(0.5), math.log(2.0)))
    return values.astype(jnp.float32)


def draw_measured(key, part):
    keys = jax.random.split(jax.random.fold_in(key, 37), 6)
    two_pi = 2.0 * math.pi
    wave_z = jax.random.uniform(keys[0], (4,), jnp.float32, 12.0, 64.0)
    wave_y = jax.random.uniform(keys[1], (4,), jnp.float32, 16.0, 256.0)
    wave_x = jax.random.uniform(keys[2], (4,), jnp.float32, 16.0, 256.0)
    phases = jax.random.uniform(keys[3], (4, 3), jnp.float32, 0.0, two_pi)
    plane_pos = jnp.arange(NZ, dtype=jnp.float32)
    row_pos = jnp.arange(NY, dtype=jnp.float32)
    col_pos = jnp.arange(NXT, dtype=jnp.float32)
    smooth = jnp.zeros((NZ, NY, NXT), jnp.float32)
    for term in range(4):
        along_z = jnp.cos(two_pi * plane_pos / wave_z[term] + phases[term, 0])
        along_y = jnp.cos(two_pi * row_pos / wave_y[term] + phases[term, 1])
        along_x = jnp.cos(two_pi * col_pos / wave_x[term] + phases[term, 2])
        smooth = smooth + along_z[:, None, None] * along_y[None, :, None] * along_x[None, None, :]
    brightness = jnp.exp(jax.random.uniform(keys[4], (VIEWS, 1, 1, 1), jnp.float32, math.log(0.7), math.log(1.4)))
    truth = jnp.exp(0.3 * smooth)
    rough = jnp.exp(jax.random.uniform(keys[5], (VIEWS, NZ, NY, NXT), jnp.float32, math.log(0.5), math.log(2.0)))
    return (brightness * truth[None] * rough).astype(jnp.bfloat16)


def draw_offsets(key, part):
    first_key, second_key, third_key = jax.random.split(jax.random.fold_in(key, 11), 3)
    values = jax.random.randint(first_key, (VIEWS, 2), -SHIFT, SHIFT + 1, dtype=jnp.int32)
    top_view = jax.random.randint(second_key, (), 0, VIEWS, dtype=jnp.int32)
    low_view = jax.random.randint(third_key, (), 0, VIEWS, dtype=jnp.int32)
    values = values.at[top_view, 0].set(SHIFT)
    values = values.at[low_view, 1].set(-SHIFT)
    return values


def draw_coverage(key, part):
    first_key, second_key, third_key = jax.random.split(jax.random.fold_in(key, 23), 3)
    levels = jax.random.randint(first_key, (VIEWS, 1), 1, 4, dtype=jnp.int32)
    coin_draws = jax.random.randint(second_key, (VIEWS, TILES), 0, 4, dtype=jnp.int32)
    chosen = jax.random.randint(third_key, (TILES,), 0, VIEWS, dtype=jnp.int32)
    view_ids = jnp.arange(VIEWS, dtype=jnp.int32)[:, None]
    random_part = (coin_draws < levels).astype(jnp.int32)
    forced_part = (view_ids == chosen[None, :]).astype(jnp.int32)
    return jnp.maximum(random_part, forced_part)


def shard_levels(key, shape, cuts, least, largest):
    factor_of = 1.0
    for dim, blocks in cuts:
        steps = jax.random.uniform(jax.random.fold_in(jax.random.fold_in(key, 6), dim), (blocks,), jnp.float32, least / len(cuts), largest / len(cuts))
        factor_of = factor_of * jnp.repeat(jnp.exp(steps), shape[dim] // blocks).reshape((-1,) + (1,) * (len(shape) - 1 - dim))
    return factor_of


def setup_inputs(seed: int = 0) -> dict:
    splits = jax.random.split(jax.random.key(seed), 7)
    return {
        "estimate": draw_estimate(jax.random.fold_in(splits[6], 71), 0),
        "measured": draw_measured(jax.random.fold_in(splits[6], 71), 0),
        "psf_z": jnp.clip(jnp.exp(math.log(1.0) - 2.9957323 * jax.random.uniform(splits[2], (VIEWS, KZ), jnp.float32) ** shard_levels(splits[2], (VIEWS, KZ), ((0, 2),), -0.2, 0.2)), 0.05, 1.0),
        "psf_xy": jnp.clip(jnp.exp(math.log(1.0) - 2.3025851 * jax.random.uniform(splits[3], (VIEWS, 2, KXY), jnp.float32) ** shard_levels(splits[3], (VIEWS, 2, KXY), ((0, 2),), -0.2, 0.2)), 0.1, 1.0),
        "offsets": draw_offsets(jax.random.fold_in(splits[6], 71), 0),
        "coverage": draw_coverage(jax.random.fold_in(splits[6], 71), 0),
    }


EXACT_MATMUL = lax.Precision.HIGHEST


def band_matrix(kernel, n_in, n_out, lead_offset):
    count_taps = kernel.shape[-1]
    rows_in = jnp.arange(n_in, dtype=jnp.int32)[:, None]
    rows_out = jnp.arange(n_out, dtype=jnp.int32)[None, :]
    tap_ids = jnp.arange(count_taps, dtype=jnp.int32)[:, None, None]
    selector = ((rows_in - rows_out + lead_offset)[None] == tap_ids).astype(jnp.float32)
    return jnp.tensordot(kernel, selector, axes=1, precision=EXACT_MATMUL)


def place_kernel(kernel, shift_value):
    count_taps = kernel.shape[0]
    positions = jnp.arange(count_taps + 2 * SHIFT, dtype=jnp.int32)[None, :]
    tap_ids = jnp.arange(count_taps, dtype=jnp.int32)[:, None]
    selector = (positions == tap_ids + SHIFT + shift_value.astype(jnp.int32)).astype(jnp.float32)
    return jnp.dot(kernel, selector, precision=EXACT_MATMUL)


def shifted_sum(object_volume, kernel, axis):
    count_taps = kernel.shape[0]
    margin = (count_taps - 1) // 2
    size_axis = object_volume.shape[axis]
    pad_widths = [(0, 0), (0, 0), (0, 0)]
    pad_widths[axis] = (margin, margin)
    padded = jnp.pad(object_volume, pad_widths)
    result = jnp.zeros_like(object_volume)
    for tap_index in range(count_taps):
        result = result + kernel[tap_index] * lax.slice_in_dim(padded, tap_index, tap_index + size_axis, axis=axis)
    return result


def reference(estimate, measured, psf_z, psf_xy, offsets, coverage):
    current = estimate
    view_count = jnp.repeat(jnp.sum(coverage, axis=0), TY).astype(jnp.float32)
    for iteration in range(ITERS):
        log_total = jnp.zeros_like(current)
        for view_index in range(VIEWS):
            z_kernel = psf_z[view_index] / jnp.sum(psf_z[view_index])
            y_kernel = psf_xy[view_index, 0] / jnp.sum(psf_xy[view_index, 0])
            x_kernel = psf_xy[view_index, 1] / jnp.sum(psf_xy[view_index, 1])
            depth_banded = band_matrix(z_kernel, NZ, NZ, RZ)
            y_taps = place_kernel(y_kernel, offsets[view_index, 0])
            x_taps = place_kernel(x_kernel, offsets[view_index, 1])
            blurred = jnp.einsum("ab,ayx->byx", depth_banded, current, precision=EXACT_MATMUL)
            blurred = shifted_sum(blurred, y_taps, 1)
            blurred = shifted_sum(blurred, x_taps, 2)
            measurement_ratios = measured[view_index].astype(jnp.float32) / blurred
            updated_estimate = jnp.einsum("ab,byx->ayx", depth_banded, measurement_ratios, precision=EXACT_MATMUL)
            updated_estimate = shifted_sum(updated_estimate, jnp.flip(y_taps), 1)
            updated_estimate = shifted_sum(updated_estimate, jnp.flip(x_taps), 2)
            covered = jnp.repeat(coverage[view_index], TY).astype(jnp.float32)
            log_total = log_total + covered[None, :, None] * jnp.log(updated_estimate)
        current = current * jnp.exp(log_total / view_count[None, :, None])
    return current
```

```python
import functools

import jax
import jax.numpy as jnp
from jax import lax
from jax.experimental import pallas as pl
from jax.experimental.pallas import tpu as pltpu
from jax.sharding import PartitionSpec as P

SHIFT = 4
ITERS = 2
LANES = 128
CHUNK = 8
EDGE = 16

f32, bf16 = jnp.float32, jnp.bfloat16
VMEM = functools.partial(pl.BlockSpec, memory_space=pltpu.VMEM)
SMEM = functools.partial(pl.BlockSpec, memory_space=pltpu.SMEM)


def lanes_of(value):
    return lax.broadcasted_iota(jnp.int32, value.shape, value.ndim - 1)


def edge_lanes(value, view, views):
    lane = lanes_of(value)
    keep = ((lane >= LANES - EDGE) & (view > 0)) | ((lane < EDGE) & (view < views - 1))
    return jnp.where(keep, value, 0.0)


def useful(value):
    lane = lanes_of(value)
    return jnp.where((lane >= LANES - EDGE) | (lane < EDGE), value, 0.0)


def rolled(value, shift):
    return value if shift % LANES == 0 else pltpu.roll(value, shift % LANES, value.ndim - 1)


def join_edges(left, right):
    return jnp.where(lanes_of(left) >= LANES // 2, left, right)


def split(value):
    high = value.astype(bf16)
    return high, (value - high.astype(f32)).astype(bf16)


def dot(a, b):
    return lax.dot_general(a, b, (((1,), (0,)), ((), ())), preferred_element_type=f32)


def pack_views_kernel(views, at, first, last, *refs):
    pieces = refs[: 3 * (views - 1)]
    psf_z, psf_xy, offsets, coverage = refs[3 * (views - 1) : 3 * (views - 1) + 4]
    outs = refs[3 * (views - 1) + 4 :]
    taps_out = outs[-1]
    half = first.shape[0] // 2
    own = useful(join_edges(last[...], first[...]))
    for step in range(views - 1):
        main, left, right = pieces[3 * step : 3 * step + 3]
        outs[2 * step][...] = main[0]
        image = useful(join_edges(left[0].astype(f32), right[0].astype(f32)))
        tile = own + rolled(image, 2 * EDGE)
        tile = tile[:half] + rolled(tile[half:], LANES // 2)
        outs[2 * step + 1][...] = tile.astype(bf16)
    taps_out[...] = jnp.zeros_like(taps_out)
    taps_out[0:1, : psf_z.shape[1]] = psf_z[...]
    taps_out[1:3, : psf_xy.shape[2]] = psf_xy[0]
    lane = lax.broadcasted_iota(jnp.int32, (1, LANES), 1)
    row = jnp.where(lane == 0, offsets[0, 0].astype(f32), 0.0)
    row = jnp.where(lane == 1, offsets[0, 1].astype(f32), row)
    taps_out[3:4, :] = jnp.where(lane == 2, coverage[0, 0].astype(f32), row)


def pack_views(at, estimate, measured, psf_z, psf_xy, offsets, coverage, views):
    planes, rows, cols = estimate.shape
    tiles = cols // LANES
    specs = [
        pl.BlockSpec((planes, rows, LANES), lambda i, at: (0, 0, 0)),
        pl.BlockSpec((planes, rows, LANES), lambda i, at: (0, 0, tiles - 1)),
    ]
    arrays = [estimate, estimate]
    outs, out_specs = [], []

    def whole(shape):
        return pl.BlockSpec(shape, lambda i, at: (0,) * len(shape))

    for step in range(1, views):

        def goal(at, step=step):
            return lax.rem(at[0] + step, views)

        specs += [
            pl.BlockSpec((1, planes, rows, cols), lambda i, at, goal=goal: (0, 0, 0, goal(at))),
            pl.BlockSpec(
                (1, planes, rows, LANES), lambda i, at, goal=goal: (0, 0, 0, jnp.maximum(goal(at) * tiles - 1, 0))
            ),
            pl.BlockSpec(
                (1, planes, rows, LANES),
                lambda i, at, goal=goal: (0, 0, 0, jnp.minimum((goal(at) + 1) * tiles, views * tiles - 1)),
            ),
        ]
        arrays += [measured] * 3
        for shape in ((planes, rows, cols), (planes // 2, rows, LANES)):
            outs.append(jax.ShapeDtypeStruct(shape, bf16))
            out_specs.append(whole(shape))
    specs += [whole(psf_z.shape), whole(psf_xy.shape), SMEM(), SMEM()]
    arrays += [psf_z, psf_xy, offsets, coverage]
    outs.append(jax.ShapeDtypeStruct((8, LANES), f32))
    out_specs.append(whole((8, LANES)))
    return pl.pallas_call(
        functools.partial(pack_views_kernel, views),
        grid_spec=pltpu.PrefetchScalarGridSpec(
            num_scalar_prefetch=1, grid=(1,), in_specs=specs, out_specs=out_specs
        ),
        out_shape=outs,
    )(at, *arrays)


def field_places(views, cols):
    base = (1 + views) * cols
    width = base + LANES * -(-(1 + views) // 4)
    return [(base + LANES * (f // 4), 2 * EDGE * (f % 4)) for f in range(1 + views)], width


def view_edges(packed, views, view, estimate):
    tile = packed.astype(f32)
    tile = jnp.concatenate([tile, rolled(tile, LANES // 2)], axis=0)
    tile = tile if estimate else rolled(tile, -2 * EDGE)
    return edge_lanes(tile, view, views)


def estimate_edges(from_left, from_right, views, view):
    left = view_edges(from_left[...], views, view, True)
    right = view_edges(from_right[...], views, view, True)
    return join_edges(left, right)


def pack_rows_kernel(views, at, *refs):
    down_out, up_out = refs[-2:]
    view = at[0]
    per_side = 4 + 2 * (views - 1)
    for side, out in enumerate((down_out, up_out)):
        mine = refs[side * per_side : (side + 1) * per_side]
        estimate, main, left, right = mine[:4]
        sent, packed = mine[4 : 4 + views - 1], mine[4 + views - 1 :]
        cols = estimate.shape[-1]
        places, width = field_places(views, cols)
        edges = [estimate_edges(packed[0], packed[views - 2], views, view)]
        edges.append(edge_lanes(join_edges(left[0].astype(f32), right[0].astype(f32)), view, views))
        out[:, :, :cols] = estimate[...].astype(bf16)
        out[:, :, cols : 2 * cols] = main[0]
        for step in range(views - 1):
            out[:, :, (2 + step) * cols : (3 + step) * cols] = sent[step][...]
            edges.append(view_edges(packed[step][...], views, view, False))
        tiles = {}
        for (lane, shift), edge in zip(places, edges):
            edge = rolled(edge, shift)
            tiles[lane] = tiles[lane] + edge if lane in tiles else edge
        for lane, tile in tiles.items():
            out[:, :, lane : lane + LANES] = tile.astype(bf16)


def pack_rows(at, estimate, measured, sent, packed, views):
    planes, rows, cols = estimate.shape
    tiles = cols // LANES
    _, width = field_places(views, cols)
    specs, arrays = [], []
    for block in (0, rows // CHUNK - 1):
        specs += [
            pl.BlockSpec((planes, CHUNK, cols), lambda i, at, block=block: (0, block, 0)),
            pl.BlockSpec((1, planes, CHUNK, cols), lambda i, at, block=block: (0, 0, block, at[0])),
            pl.BlockSpec(
                (1, planes, CHUNK, LANES),
                lambda i, at, block=block: (0, 0, block, jnp.maximum(at[0] * tiles - 1, 0)),
            ),
            pl.BlockSpec(
                (1, planes, CHUNK, LANES),
                lambda i, at, block=block: (0, 0, block, jnp.minimum((at[0] + 1) * tiles, views * tiles - 1)),
            ),
        ]
        specs += [pl.BlockSpec((planes, CHUNK, cols), lambda i, at, block=block: (0, block, 0))] * (views - 1)
        specs += [pl.BlockSpec((planes // 2, CHUNK, LANES), lambda i, at, block=block: (0, block, 0))] * (views - 1)
        arrays += [estimate, measured, measured, measured, *sent, *packed]
    shape = (planes, CHUNK, width)
    return pl.pallas_call(
        functools.partial(pack_rows_kernel, views),
        grid_spec=pltpu.PrefetchScalarGridSpec(
            num_scalar_prefetch=1,
            grid=(1,),
            in_specs=specs,
            out_specs=[pl.BlockSpec(shape, lambda i, at: (0, 0, 0))] * 2,
        ),
        out_shape=[jax.ShapeDtypeStruct(shape, bf16)] * 2,
    )(at, *arrays)


def build_filters(taps, taps_row, sizes, row_filter, col_filter, work):
    planes, count_z, count = sizes
    reach = (count - 1) // 2
    window = 2 * CHUNK
    span = planes * window
    width = 2 * span
    total_z = jnp.sum(taps_row[0:1, :], axis=1, keepdims=True)
    total_y = jnp.sum(taps_row[1:2, :], axis=1, keepdims=True)
    total_x = jnp.sum(taps_row[2:3, :], axis=1, keepdims=True)
    lane = lax.broadcasted_iota(jnp.int32, (CHUNK, width), 1) // window
    base = (count_z - 1) // 2
    y_in = lax.broadcasted_iota(jnp.int32, (CHUNK, span), 1) % window
    y_out = lax.broadcasted_iota(jnp.int32, (CHUNK, span), 0)
    for way in range(2):
        strip = jnp.zeros((CHUNK, width), f32)
        for d in range(2 * planes - 1):
            tap = base - (planes - 1) + d if way == 0 else base + (planes - 1) - d
            strip = jnp.where(lane == d, taps[0, tap], strip)
        strip = strip / total_z
        band = jnp.zeros((CHUNK, span), f32)
        for c in range(count):
            wanted = c if way == 0 else count - 1 - c
            band = jnp.where(y_in - y_out == wanted, taps[1, c], band)
        band = band / total_y
        for z in range(planes):
            start = (planes - 1 - z) * window
            piece = strip if start == 0 else pltpu.roll(strip, width - start, 1)
            work[z * CHUNK : (z + 1) * CHUNK, :] = piece[:, :span] * band
        high, low = split(work[...])
        row_filter[2 * way] = high
        row_filter[2 * way + 1] = low
    offset = taps[3, 1].astype(jnp.int32)
    col_in = lax.broadcasted_iota(jnp.int32, (2 * LANES, LANES), 0)
    col_out = lax.broadcasted_iota(jnp.int32, (2 * LANES, LANES), 1)
    half = LANES // 2
    for way in range(2):
        if way == 0:
            index = col_in - col_out - (half - reach) - offset
        else:
            index = col_out - col_in + (half + reach) - offset
        band = jnp.zeros((2 * LANES, LANES), f32)
        for c in range(count):
            band = jnp.where(index == c, taps[2, c], band)
        high, low = split(band / total_x)
        col_filter[way, :, :LANES] = high
        col_filter[way, :, LANES:] = low


def forward_and_back(views, taps, frame, images, ratios, high, low, logs, row_filter, col_filter, halo, emit):
    planes, _, width = frame.shape
    cols = width - 2 * LANES
    tiles = cols // LANES
    ext = ratios.shape[2]
    rows = ext - CHUNK
    block = planes * CHUNK
    window = 2 * CHUNK
    span = planes * window

    def pieces(total):
        return [(i, min(2 * LANES, total - i)) for i in range(0, total, 2 * LANES)]

    def forward_chunk(j, _):
        start = pl.multiple_of(j * CHUNK, CHUNK)
        for lane, size in pieces(width):
            part = frame[:, pl.ds(start, window), lane : lane + size].reshape(span, size)
            part_high, part_low = split(part)
            for k in range(views):
                wide = dot(row_filter[k, 0], part_high) + dot(row_filter[k, 1], part_high)
                wide = wide + dot(row_filter[k, 0], part_low)
                wide_high, wide_low = split(wide)
                spot = pl.ds(pl.multiple_of(j * block, block), block)
                high[k, spot, lane : lane + size] = wide_high
                low[k, spot, lane : lane + size] = wide_low
        return 0

    lax.fori_loop(0, ext // CHUNK, forward_chunk, 0)

    for k in range(views):
        for b in range(tiles + 1):
            first = slice(b * LANES, (b + 2) * LANES)
            here = slice(b * LANES, (b + 1) * LANES)
            both = dot(high[k, :, first], col_filter[k, 0])
            blurred = both[:, :LANES] + both[:, LANES:] + dot(low[k, :, first], col_filter[k, 0, :, :LANES])
            for j in range(ext // CHUNK):
                value = blurred[j * block : (j + 1) * block].reshape(planes, CHUNK, LANES)
                spot = slice(j * CHUNK, (j + 1) * CHUNK)
                image = images[k, :, spot, here].astype(f32)
                ratios[k, :, spot, here] = jnp.where(value > 0.0, image / value, 0.0)

    def back_chunk(i, _):
        start = pl.multiple_of(i * CHUNK, CHUNK)
        for k in range(views):
            for lane, size in pieces(width - LANES):
                part = ratios[k, :, pl.ds(start, window), lane : lane + size].reshape(span, size)
                part_high, part_low = split(part)
                wide = dot(row_filter[k, 2], part_high) + dot(row_filter[k, 3], part_high)
                wide = wide + dot(row_filter[k, 2], part_low)
                wide_high, wide_low = split(wide)
                spot = pl.ds(pl.multiple_of(i * block, block), block)
                high[k, spot, lane : lane + size] = wide_high
                low[k, spot, lane : lane + size] = wide_low
        return 0

    lax.fori_loop(0, rows // CHUNK, back_chunk, 0)

    count = taps[0][3, 2]
    for k in range(1, views):
        count = count + taps[k][3, 2]
    deep = rows // CHUNK * block
    for b in range(-1 if halo else 0, tiles + 1 if halo else tiles):
        if b < 0:
            first, depth = slice(0, LANES), slice(LANES, 2 * LANES)
        elif b == tiles:
            first, depth = slice(b * LANES, (b + 1) * LANES), slice(0, LANES)
        else:
            first, depth = slice(b * LANES, (b + 2) * LANES), slice(0, 2 * LANES)
        for k in range(views):
            both = dot(high[k, :deep, first], col_filter[k, 1, depth, :])
            back = both[:, :LANES] + both[:, LANES:] + dot(low[k, :deep, first], col_filter[k, 1, depth, :LANES])
            term = taps[k][3, 2] * jnp.log(back)
            if views == 1:
                total = term
            elif k == 0:
                logs[...] = term
            elif k < views - 1:
                logs[...] += term
            else:
                total = logs[...] + term
        factor = jnp.exp(total / count)
        for i in range(rows // CHUNK):
            now = frame[:, CHUNK + i * CHUNK : 2 * CHUNK + i * CHUNK, (b + 1) * LANES : (b + 2) * LANES]
            by = factor[i * block : (i + 1) * block].reshape(planes, CHUNK, LANES)
            emit(b, i, jnp.where(now > 0.0, now * by, 0.0))


def first_kernel(views, sizes, at, *refs):
    refs = list(refs)

    def take(n):
        out = refs[:n]
        del refs[:n]
        return out

    estimate, main, left, right = take(4)
    sent, packed = take(views - 1), take(views - 1)
    above, below = take(2)
    taps, taps_rows = take(views), take(views)
    current, edge, down_out, up_out, images, row_filter, col_filter = take(7)
    frame, ratios, high, low, logs, work, shifted = take(7)
    planes, rows, cols = estimate.shape
    tiles = cols // LANES
    view = at[0]
    for k in range(views):
        build_filters(taps[k], taps_rows[k], sizes, row_filter.at[k], col_filter.at[k], work)
    places, _ = field_places(views, cols)
    chunks = rows // CHUNK

    def halo_tile(ref, field, index):
        if 0 <= index < tiles:
            return ref[:, :, field * cols + index * LANES : field * cols + (index + 1) * LANES].astype(f32)
        lane, shift = places[field]
        return rolled(ref[:, :, lane : lane + LANES].astype(f32), -shift)

    def inner(value):
        return jnp.where(lanes_of(value) >= LANES // 2, value, 0.0)

    def outer(value):
        return jnp.where(lanes_of(value) < LANES // 2, value, 0.0)

    for spot, ref in ((slice(0, CHUNK), above), (slice(CHUNK + rows, 2 * CHUNK + rows), below)):
        for b in range(tiles):
            frame[:, spot, (b + 1) * LANES : (b + 2) * LANES] = halo_tile(ref, 0, b)
        tile = useful(halo_tile(ref, 0, -1))
        frame[:, spot, :LANES] = inner(tile)
        frame[:, spot, (tiles + 1) * LANES :] = outer(tile)
    for q in range(chunks):
        spot, here = slice(CHUNK + q * CHUNK, 2 * CHUNK + q * CHUNK), slice(q * CHUNK, (q + 1) * CHUNK)
        frame[:, spot, LANES : LANES + cols] = estimate[:, here, :]
        tile = estimate_edges(packed[0].at[:, here, :], packed[views - 2].at[:, here, :], views, view)
        frame[:, spot, :LANES] = inner(tile)
        frame[:, spot, (tiles + 1) * LANES :] = outer(tile)

    def image_tile(k, q, index):
        if q == 0:
            return useful(halo_tile(above, 1 + k, index)) if not 0 <= index < tiles else halo_tile(above, 1 + k, index)
        if q == chunks + 1:
            return useful(halo_tile(below, 1 + k, index)) if not 0 <= index < tiles else halo_tile(below, 1 + k, index)
        here = slice((q - 1) * CHUNK, q * CHUNK)
        if 0 <= index < tiles:
            lane = slice(index * LANES, (index + 1) * LANES)
            return (main[0, :, here, lane] if k == 0 else sent[k - 1][:, here, lane]).astype(f32)
        if k == 0:
            tile = join_edges(left[0, :, here, :].astype(f32), right[0, :, here, :].astype(f32))
            return edge_lanes(tile, view, views)
        return view_edges(packed[k - 1][:, here, :], views, view, False)

    lane = lax.broadcasted_iota(jnp.int32, (planes, CHUNK, LANES), 2)
    row = lax.broadcasted_iota(jnp.int32, (planes, CHUNK, LANES), 1)
    for k in range(views):
        lead = SHIFT - taps[k][3, 0].astype(jnp.int32)
        turn = lax.rem(CHUNK - lead, CHUNK)
        for q in range(chunks + 2):
            after = rolled(image_tile(k, q, -1), LANES // 2)
            for b in range(tiles + 1):
                before, after = after, rolled(image_tile(k, q, b), LANES // 2)
                value = jnp.where(lane < LANES // 2, before, after)
                value = pltpu.roll(value, turn, 1)
                here = slice(b * LANES, (b + 1) * LANES)
                if q > 0:
                    spot = slice((q - 1) * CHUNK, q * CHUNK)
                    images[k, :, spot, here] = jnp.where(row < CHUNK - lead, shifted[:, :, here], value).astype(bf16)
                shifted[:, :, here] = value

    def emit(b, i, value):
        here = slice(i * CHUNK, (i + 1) * CHUNK)
        if 0 <= b < tiles:
            current[:, here, b * LANES : (b + 1) * LANES] = value
            spot = slice(b * LANES, (b + 1) * LANES)
        else:
            lane = lanes_of(value)
            if b < 0:
                edge[:, here, :] = jnp.where(lane >= LANES - CHUNK, value, 0.0)
                return
            value = jnp.where(lane < CHUNK, value, edge[:, here, :])
            edge[:, here, :] = value
            spot = slice(cols, cols + LANES)
        if i == 0:
            down_out[:, :, spot] = value.astype(bf16)
        if i == chunks - 1:
            up_out[:, :, spot] = value.astype(bf16)

    forward_and_back(views, taps, frame, images, ratios, high, low, logs, row_filter, col_filter, True, emit)


def second_kernel(views, *refs):
    current, edge, above, below, images, row_filter, col_filter = refs[:7]
    taps = refs[7 : 7 + views]
    restored = refs[7 + views]
    frame, ratios, high, low, logs = refs[8 + views :]
    planes, rows, cols = current.shape

    def sides(spot, tile):
        lane = lanes_of(tile)
        frame[:, spot, :LANES] = jnp.where(lane >= LANES - CHUNK, tile, 0.0)
        frame[:, spot, LANES + cols :] = jnp.where(lane < CHUNK, tile, 0.0)

    for spot, ref in ((slice(0, CHUNK), above), (slice(CHUNK + rows, 2 * CHUNK + rows), below)):
        frame[:, spot, LANES : LANES + cols] = ref[:, :, :cols].astype(f32)
        sides(spot, ref[:, :, cols:].astype(f32))
    for q in range(rows // CHUNK):
        spot, here = slice(CHUNK + q * CHUNK, 2 * CHUNK + q * CHUNK), slice(q * CHUNK, (q + 1) * CHUNK)
        frame[:, spot, LANES : LANES + cols] = current[:, here, :]
        sides(spot, edge[:, here, :])

    def emit(b, i, value):
        restored[:, i * CHUNK : (i + 1) * CHUNK, b * LANES : (b + 1) * LANES] = value

    forward_and_back(views, taps, frame, images, ratios, high, low, logs, row_filter, col_filter, False, emit)


def scratch(planes, rows, cols, views):
    ext = rows + CHUNK
    return [
        pltpu.VMEM((planes, rows + 2 * CHUNK, cols + 2 * LANES), f32),
        pltpu.VMEM((views, planes, ext, cols + LANES), f32),
        pltpu.VMEM((views, planes * ext, cols + 2 * LANES), bf16),
        pltpu.VMEM((views, planes * ext, cols + 2 * LANES), bf16),
        pltpu.VMEM((planes * rows, LANES), f32),
    ]


def body(views, estimate, measured, psf_z, psf_xy, offsets, coverage):
    planes, rows, cols = estimate.shape
    tiles = cols // LANES
    sizes = (planes, psf_z.shape[1], psf_xy.shape[2])
    at = lax.axis_index("view").astype(jnp.int32).reshape(1)
    *pieces, own_taps = pack_views(at, estimate, measured, psf_z, psf_xy, offsets, coverage, views)

    def across(x, step):
        return lax.ppermute(x, "view", [(i, (i + step) % views) for i in range(views)])

    steps = range(1, views)
    taps = [own_taps] + [across(own_taps, step) for step in steps]
    packed = [across(pieces[2 * (step - 1) + 1], step) for step in steps]
    sent = [across(pieces[2 * (step - 1)], step) for step in steps]

    size = lax.axis_size("tile")
    later = [(i, i + 1) for i in range(size - 1)]
    earlier = [(i + 1, i) for i in range(size - 1)]
    to_earlier, to_later = pack_rows(at, estimate, measured, sent, packed, views)
    above = lax.ppermute(to_later, "tile", later)
    below = lax.ppermute(to_earlier, "tile", earlier)

    def whole(shape):
        return pl.BlockSpec(shape, lambda i, at: (0,) * len(shape))

    ext = rows + CHUNK
    outs = [
        jax.ShapeDtypeStruct((planes, rows, cols), f32),
        jax.ShapeDtypeStruct((planes, rows, LANES), f32),
        jax.ShapeDtypeStruct((planes, CHUNK, cols + LANES), bf16),
        jax.ShapeDtypeStruct((planes, CHUNK, cols + LANES), bf16),
        jax.ShapeDtypeStruct((views, planes, ext, cols + LANES), bf16),
        jax.ShapeDtypeStruct((views, 4, planes * CHUNK, 2 * planes * CHUNK), bf16),
        jax.ShapeDtypeStruct((views, 2, 2 * LANES, 2 * LANES), bf16),
    ]
    in_specs = [
        whole(estimate.shape),
        pl.BlockSpec((1, planes, rows, cols), lambda i, at: (0, 0, 0, at[0])),
        pl.BlockSpec((1, planes, rows, LANES), lambda i, at: (0, 0, 0, jnp.maximum(at[0] * tiles - 1, 0))),
        pl.BlockSpec(
            (1, planes, rows, LANES), lambda i, at: (0, 0, 0, jnp.minimum((at[0] + 1) * tiles, views * tiles - 1))
        ),
    ]
    in_specs += [whole(x.shape) for x in (*sent, *packed, above, below)]
    in_specs += [SMEM()] * views + [whole((8, LANES))] * views
    current, edge, to_earlier, to_later, images, row_filter, col_filter = pl.pallas_call(
        functools.partial(first_kernel, views, sizes),
        grid_spec=pltpu.PrefetchScalarGridSpec(
            num_scalar_prefetch=1,
            grid=(1,),
            in_specs=in_specs,
            out_specs=[whole(x.shape) for x in outs],
            scratch_shapes=scratch(planes, rows, cols, views)
            + [
                pltpu.VMEM((planes * CHUNK, 2 * planes * CHUNK), f32),
                pltpu.VMEM((planes, CHUNK, cols + LANES), f32),
            ],
        ),
        out_shape=outs,
    )(at, estimate, measured, measured, measured, *sent, *packed, above, below, *taps, *taps)

    above = lax.ppermute(to_later, "tile", later)
    below = lax.ppermute(to_earlier, "tile", earlier)
    return pl.pallas_call(
        functools.partial(second_kernel, views),
        in_specs=[VMEM()] * 7 + [SMEM()] * views,
        out_specs=VMEM(),
        out_shape=jax.ShapeDtypeStruct((planes, rows, cols), f32),
        scratch_shapes=scratch(planes, rows, cols, views),
    )(current, edge, above, below, images, row_filter, col_filter, *taps)


def solution(mesh):
    placed = (
        P(None, "tile", "view"),
        P("view", None, "tile", None),
        P("view", None),
        P("view", None, None),
        P("view", None),
        P("view", "tile"),
    )
    return jax.shard_map(
        functools.partial(body, mesh.shape["view"]),
        mesh=mesh,
        in_specs=placed,
        out_specs=P(None, "tile", "view"),
        check_vma=False,
    )
```
